32 devices in a mesh: lvl: 4 (over y, x), gz: 4 (over z), gy: 2 (over core).
Axes of the slice: x: 2, y: 2, z: 4, core: 2. Of those that a mesh axis runs over, the one named last changes fastest.
Arguments:
- fine_field: float32 [32, 512, 1024], P('gz', 'gy', 'lvl'), may hold values from -1.2 to 1.2
- noise_pair: float32 [2, 32, 512, 1024], P(None, 'gz', 'gy', 'lvl'), may hold values from -4 to 4
Outputs:
- fine_next: float32 [32, 512, 1024], P('gz', 'gy', 'lvl')
- correction: float32 [16, 256, 512], P('gz', 'gy', 'lvl')
The draws below stay inside these ranges and needn't reach their ends.
All inputs are finite; a program needn't handle non-finite values.
Results may differ from the reference program's by a relative error of at most 0.00014.
Values sent between devices are 32-bit elements; how exact they have to be, the bound alone decides.
A program may use at most 64 MiB of HBM per device.

```python
import jax
import jax.numpy as jnp

NX = 32
NY = 512
NZ = 1024


def block_scale(rng, extent, cuts, least, largest):
    def one(axis_at, shards_of):
        draws = jax.random.uniform(jax.random.fold_in(jax.random.fold_in(rng, 6), axis_at), (shards_of,), jnp.float32, least / len(cuts), largest / len(cuts))
        return jnp.repeat(jnp.exp(draws), extent[axis_at] // shards_of).reshape((-1,) + (1,) * (len(extent) - axis_at - 1))

    level = one(*cuts[0])
    for cut in cuts[1:]:
        level = level * one(*cut)
    return level


def scatter_about(stream_key, extent, deviation, bound, pieces=(), dtype=jnp.bfloat16):
    values = jax.random.normal(stream_key, extent, jnp.float32) * deviation
    if len(pieces) > 0:
        values = block_scale(stream_key, extent, pieces, -0.22, 0.18) * values
    return jnp.clip(values, min=-bound, max=bound).astype(dtype)


def setup_inputs(seed: int = 0) -> dict:
    streams_of = jax.random.split(jax.random.key(seed), 3)
    return {
        "fine_field": jnp.clip(jax.random.uniform(streams_of[0], (NX, NY, NZ), jnp.float32, -1.2, 1.2) * block_scale(streams_of[0], (NX, NY, NZ), ((0, 4), (1, 2), (2, 4)), -0.4, 0.0), -1.2, 1.2),
        "noise_pair": scatter_about(streams_of[1], (2, NX, NY, NZ), 1.0, 4.0, ((1, 4), (2, 2), (3, 4)), jnp.float32),
    }


noise_amp = 0.3


def advance(field, forcing, spread, react):
    beside = jnp.roll(field, 1, 0) + jnp.roll(field, -1, 0)
    beside = beside + jnp.roll(field, 1, 1) + jnp.roll(field, -1, 1)
    beside = beside + jnp.roll(field, 1, 2) + jnp.roll(field, -1, 2)
    return field + spread * (beside - 6.0 * field) + react * (field - field * field * field) + noise_amp * forcing


def coarsen(values):
    first, second, third = values.shape
    blocks = values.reshape(first // 2, 2, second // 2, 2, third // 2, 2)
    return blocks.sum(axis=(1, 3, 5)) * 0.125


def reference(fine_field, noise_pair):
    middle = advance(fine_field, noise_pair[0], 0.15, 0.1)
    fine_next = advance(middle, noise_pair[1], 0.15, 0.1)
    coarse_start = coarsen(fine_field)
    coarse_noise = coarsen(noise_pair[0] + noise_pair[1])
    coarse_next = advance(coarse_start, coarse_noise, 0.075, 0.2)
    return fine_next, coarsen(fine_next) - coarse_next
```

```python
import functools

import jax
import jax.numpy as jnp
from jax import lax
from jax.experimental import pallas as pl
from jax.experimental.pallas import tpu as pltpu
from jax.sharding import PartitionSpec as P

noise_amp = 0.3
lanes = 128
pad = 8
steps = 4


def remote(src, dst, send, recv, axis, where):
    return pltpu.make_async_remote_copy(
        src_ref=src,
        dst_ref=dst,
        send_sem=send,
        recv_sem=recv,
        device_id={axis: where},
        device_id_type=pl.DeviceIdType.MESH,
    )


def pack(buf, planes, rows, wide):
    lane = lax.broadcasted_iota(jnp.int32, (rows, lanes), 1)
    both = jnp.zeros((rows, lanes), jnp.float32)
    for i in range(planes):
        head = buf[1 + i, pad : pad + rows, 0:lanes]
        tail = buf[1 + i, pad : pad + rows, wide - lanes : wide]
        if i:
            head = pltpu.roll(head, i, 1)
        both = jnp.where(lane == i, head, both)
        both = jnp.where(lane == planes + i, pltpu.roll(tail, planes + i + 1, 1), both)
    groups = lanes // (2 * planes)
    deep = rows // groups
    folded = both[0:deep]
    for g in range(1, groups):
        folded = folded + pltpu.roll(both[g * deep : (g + 1) * deep], g * 2 * planes, 1)
    return folded


def unpack(folded, out, side, planes, rows):
    groups = lanes // (2 * planes)
    deep = rows // groups
    for g in range(groups):
        part = folded if g == 0 else pltpu.roll(folded, lanes - g * 2 * planes, 1)
        out[side, g * deep : (g + 1) * deep, :] = part


def beside(buf, beyond, i, r0, rows, planes, wide):
    y = buf[i, pl.ds(r0, rows + 2 * pad), :]
    tall = rows + 2 * pad
    c = y[pad : pad + rows]
    total = pltpu.roll(y, 1, 0)[pad : pad + rows] + pltpu.roll(y, tall - 1, 0)[pad : pad + rows]
    inner = pl.ds(r0 + pad, rows)
    total = total + buf[i - 1, inner, :] + buf[i + 1, inner, :]
    lane = lax.broadcasted_iota(jnp.int32, (rows, lanes), 1)
    left = pltpu.roll(beyond[0, pl.ds(r0, rows), :], 2 * lanes - planes - (i - 1), 1)
    right = pltpu.roll(beyond[1, pl.ds(r0, rows), :], lanes - 1 - (i - 1), 1)
    back = pltpu.roll(c, 1, 1)
    ahead = pltpu.roll(c, wide - 1, 1)
    first = jnp.where(lane == 0, left, back[:, 0:lanes])
    last = jnp.where(lane == lanes - 1, right, ahead[:, wide - lanes : wide])
    if wide > lanes:
        back = jnp.concatenate([first, back[:, lanes:]], axis=1)
        ahead = jnp.concatenate([ahead[:, : wide - lanes], last], axis=1)
    else:
        back, ahead = first, last
    return c, total + back + ahead


def advanced(c, around, spread, react):
    return c + spread * (around - 6.0 * c) + react * (c - c * c * c)


def halved(block, table, tmp):
    rows = block.shape[0]
    out = None
    rest = block
    for n in range(3):
        part = rest.astype(jnp.bfloat16)
        term = jnp.dot(part, table[...], preferred_element_type=jnp.float32)
        out = term if out is None else out + term
        if n < 2:
            rest = rest - part.astype(jnp.float32)
    tmp[...] = out
    return (tmp[pl.ds(0, rows // 2, stride=2), :] + tmp[pl.ds(1, rows // 2, stride=2), :]) * 0.125


def kernel(
    sizes, field, noise, next_out, cor_out,
    vbuf, mbuf, cbuf, n0, n1, obuf, kbuf, pkv, pkm, pkc, hv, hm, hc, uv, um, uc, table, tmp,
    zs, zr, ls, lr, gs, gr, loc,
):
    nx, ny, nz = field.shape
    cx, cy, cz = nx // 2, ny // 2, nz // 2
    rows = ny // steps
    crows = rows // 2

    def ends(axis):
        me = lax.axis_index(axis)
        n = sizes[axis]
        return lax.rem(me + 1, n), lax.rem(me + n - 1, n)

    nxt = {a: ends(a)[0] for a in ("gz", "lvl", "gy")}
    prv = {a: ends(a)[1] for a in ("gz", "lvl", "gy")}

    load_v = pltpu.make_async_copy(field, vbuf.at[1 : nx + 1, pad : pad + ny, :], loc.at[0])
    load_n0 = pltpu.make_async_copy(noise.at[0], n0, loc.at[1])
    load_n1 = pltpu.make_async_copy(noise.at[1], n1, loc.at[2])
    load_v.start()
    load_n0.start()
    load_n1.start()

    barrier = pltpu.get_barrier_semaphore()
    for axis in ("gz", "lvl", "gy"):
        for side in (nxt, prv):
            pl.semaphore_signal(
                barrier, inc=1, device_id={axis: side[axis]}, device_id_type=pl.DeviceIdType.MESH
            )
    source = lax.broadcasted_iota(jnp.int32, (nz, cz), 0) // 2
    target = lax.broadcasted_iota(jnp.int32, (nz, cz), 1)
    table[...] = jnp.where(source == target, 1.0, 0.0).astype(jnp.bfloat16)
    pl.semaphore_wait(barrier, 6)

    def planes_out(src_low, src_high, buf, count, slot, where):
        up = remote(src_high, buf.at[(0,) + where], zs.at[0, slot], zr.at[0, slot], "gz", nxt["gz"])
        down = remote(src_low, buf.at[(count + 1,) + where], zs.at[1, slot], zr.at[1, slot], "gz", prv["gz"])
        up.start()
        down.start()
        return up, down

    def slabs_out(src_low, src_high, buf, count, tall, slot):
        up = remote(src_high, buf.at[1 : count + 1, 0:pad, :], gs.at[0, slot], gr.at[0, slot], "gy", nxt["gy"])
        down = remote(
            src_low, buf.at[1 : count + 1, pad + tall : 2 * pad + tall, :],
            gs.at[1, slot], gr.at[1, slot], "gy", prv["gy"],
        )
        up.start()
        down.start()
        return up, down

    def columns_out(packed, held, slot):
        up = remote(packed, held.at[0], ls.at[0, slot], lr.at[0, slot], "lvl", nxt["lvl"])
        down = remote(packed, held.at[1], ls.at[1, slot], lr.at[1, slot], "lvl", prv["lvl"])
        up.start()
        down.start()
        return up, down

    vz = []
    for c in range(steps):
        at = pl.ds(c * rows, rows)
        vz.append(
            planes_out(
                field.at[0, at, :], field.at[nx - 1, at, :], vbuf, nx, c, (pl.ds(pad + c * rows, rows), slice(None))
            )
        )
    vg = slabs_out(field.at[:, 0:pad, :], field.at[:, ny - pad : ny, :], vbuf, nx, ny, 0)

    load_v.wait()
    pkv[...] = pack(vbuf, nx, ny, nz)
    vl = columns_out(pkv, hv, 0)

    @pl.loop(0, cx * steps)
    def _(t):
        k, c = t // steps, t % steps
        at = pl.ds(pl.multiple_of(c * rows + pad, pad), rows)
        block = vbuf[2 * k + 1, at, :] + vbuf[2 * k + 2, at, :]
        cbuf[k + 1, pl.ds(pl.multiple_of(c * crows + pad, pad), crows), :] = halved(block, table, tmp)

    cin = (pl.ds(pad, cy), slice(None))
    cz_ = planes_out(cbuf.at[(1,) + cin], cbuf.at[(cx,) + cin], cbuf, cx, 2 * steps, cin)
    cg = slabs_out(cbuf.at[1 : cx + 1, pad : 2 * pad, :], cbuf.at[1 : cx + 1, cy : cy + pad, :], cbuf, cx, cy, 2)
    pkc[...] = pack(cbuf, cx, cy, cz)
    cl = columns_out(pkc, hc, 2)

    load_n0.wait()
    for copy in vg + vl:
        copy.wait_recv()
    for side in range(2):
        unpack(hv[side], uv, side, nx, ny)

    def middle(i, r0):
        c, around = beside(vbuf, uv, i, r0, rows, nx, nz)
        made = advanced(c, around, 0.15, 0.1) + noise_amp * n0[i - 1, pl.ds(r0, rows), :]
        mbuf[i, pl.ds(r0 + pad, rows), :] = made

    @pl.loop(0, (nx - 2) * steps)
    def _(t):
        middle(2 + t // steps, pl.multiple_of((t % steps) * rows, rows))

    mz = []
    for c in range(steps):
        for copy, i in zip(vz[c], (1, nx)):
            copy.wait_recv()
            middle(i, c * rows)
        where = (pl.ds(pad + c * rows, rows), slice(None))
        mz.append(planes_out(mbuf.at[(1,) + where], mbuf.at[(nx,) + where], mbuf, nx, steps + c, where))

    pkm[...] = pack(mbuf, nx, ny, nz)
    ml = columns_out(pkm, hm, 1)
    mg = slabs_out(mbuf.at[1 : nx + 1, pad : 2 * pad, :], mbuf.at[1 : nx + 1, ny : ny + pad, :], mbuf, nx, ny, 1)
    load_n1.wait()
    for copy in cz_ + cl + cg:
        copy.wait_recv()
    for side in range(2):
        unpack(hc[side], uc, side, cx, cy)
    for copy in ml + mg:
        copy.wait_recv()
    for side in range(2):
        unpack(hm[side], um, side, nx, ny)

    def finish(i, r0):
        c, around = beside(mbuf, um, i, r0, rows, nx, nz)
        made = advanced(c, around, 0.15, 0.1) + noise_amp * n1[i - 1, pl.ds(r0, rows), :]
        obuf[i - 1, pl.ds(r0, rows), :] = made

    def correct(k, r0, half):
        at = pl.ds(r0, rows)
        block = None
        for i in (2 * k, 2 * k + 1):
            term = obuf[i, at, :] - noise_amp * (n0[i, at, :] + n1[i, at, :])
            block = term if block is None else block + term
        c, around = beside(cbuf, uc, k + 1, half, crows, cx, cz)
        kbuf[k, pl.ds(half, crows), :] = halved(block, table, tmp) - advanced(c, around, 0.075, 0.2)

    @pl.loop(0, (nx - 2) * steps)
    def _(t):
        finish(2 + t // steps, pl.multiple_of((t % steps) * rows, rows))

    outs = [pltpu.make_async_copy(obuf.at[1 : nx - 1], next_out.at[1 : nx - 1], loc.at[3])]
    outs[0].start()

    @pl.loop(0, (cx - 2) * steps)
    def _(t):
        c = t % steps
        correct(1 + t // steps, pl.multiple_of(c * rows, rows), pl.multiple_of(c * crows, crows))

    outs.append(pltpu.make_async_copy(kbuf.at[1 : cx - 1], cor_out.at[1 : cx - 1], loc.at[4]))
    outs[1].start()

    for c in range(steps):
        for side, i, k in ((0, 1, 0), (1, nx, cx - 1)):
            mz[c][side].wait_recv()
            finish(i, c * rows)
            at = pl.ds(c * rows, rows)
            copy = pltpu.make_async_copy(obuf.at[i - 1, at, :], next_out.at[i - 1, at, :], loc.at[5 + 4 * c + 2 * side])
            copy.start()
            outs.append(copy)
            correct(k, c * rows, c * crows)
            at = pl.ds(c * crows, crows)
            copy = pltpu.make_async_copy(kbuf.at[k, at, :], cor_out.at[k, at, :], loc.at[6 + 4 * c + 2 * side])
            copy.start()
            outs.append(copy)

    for group in vz + mz + [vg, vl, cz_, cg, cl, ml, mg]:
        for copy in group:
            copy.wait_send()
    for copy in outs:
        copy.wait()


def on_device(sizes, fine_field, noise_pair):
    nx, ny, nz = fine_field.shape
    cx, cy, cz = nx // 2, ny // 2, nz // 2
    fold = ny // (lanes // (2 * nx))
    cfold = cy // (lanes // (2 * cx))
    f32 = jnp.float32
    whole = pl.BlockSpec(memory_space=pl.ANY)
    dma = pltpu.SemaphoreType.DMA
    return pl.pallas_call(
        functools.partial(kernel, sizes),
        out_shape=(jax.ShapeDtypeStruct((nx, ny, nz), f32), jax.ShapeDtypeStruct((cx, cy, cz), f32)),
        in_specs=[whole, whole],
        out_specs=(whole, whole),
        scratch_shapes=[
            pltpu.VMEM((nx + 2, ny + 2 * pad, nz), f32),
            pltpu.VMEM((nx + 2, ny + 2 * pad, nz), f32),
            pltpu.VMEM((cx + 2, cy + 2 * pad, cz), f32),
            pltpu.VMEM((nx, ny, nz), f32),
            pltpu.VMEM((nx, ny, nz), f32),
            pltpu.VMEM((nx, ny, nz), f32),
            pltpu.VMEM((cx, cy, cz), f32),
            pltpu.VMEM((fold, lanes), f32),
            pltpu.VMEM((fold, lanes), f32),
            pltpu.VMEM((cfold, lanes), f32),
            pltpu.VMEM((2, fold, lanes), f32),
            pltpu.VMEM((2, fold, lanes), f32),
            pltpu.VMEM((2, cfold, lanes), f32),
            pltpu.VMEM((2, ny, lanes), f32),
            pltpu.VMEM((2, ny, lanes), f32),
            pltpu.VMEM((2, cy, lanes), f32),
            pltpu.VMEM((nz, cz), jnp.bfloat16),
            pltpu.VMEM((ny // steps, cz), f32),
            dma((2, 2 * steps + 1)),
            dma((2, 2 * steps + 1)),
            dma((2, 3)),
            dma((2, 3)),
            dma((2, 3)),
            dma((2, 3)),
            dma((5 + 4 * steps,)),
        ],
        compiler_params=pltpu.CompilerParams(collective_id=0, has_side_effects=True),
    )(fine_field, noise_pair)


def solution(mesh):
    in_specs = (P("gz", "gy", "lvl"), P(None, "gz", "gy", "lvl"))
    out_specs = (P("gz", "gy", "lvl"), P("gz", "gy", "lvl"))
    sizes = dict(mesh.shape)
    return jax.shard_map(
        functools.partial(on_device, sizes), mesh=mesh, in_specs=in_specs, out_specs=out_specs, check_vma=False
    )
```

```python
import functools

import jax
import jax.numpy as jnp
from jax import lax
from jax.experimental import pallas as pl
from jax.experimental.pallas import tpu as pltpu
from jax.sharding import PartitionSpec as P

noise_amp = 0.3
lanes = 128
pad = 8
steps = 1


def remote(src, dst, send, recv, axis, where):
    return pltpu.make_async_remote_copy(
        src_ref=src,
        dst_ref=dst,
        send_sem=send,
        recv_sem=recv,
        device_id={axis: where},
        device_id_type=pl.DeviceIdType.MESH,
    )


def pack(buf, planes, rows, wide):
    lane = lax.broadcasted_iota(jnp.int32, (rows, lanes), 1)
    both = jnp.zeros((rows, lanes), jnp.float32)
    for i in range(planes):
        head = buf[1 + i, pad : pad + rows, 0:lanes]
        tail = buf[1 + i, pad : pad + rows, wide - lanes : wide]
        if i:
            head = pltpu.roll(head, i, 1)
        both = jnp.where(lane == i, head, both)
        both = jnp.where(lane == planes + i, pltpu.roll(tail, planes + i + 1, 1), both)
    groups = lanes // (2 * planes)
    deep = rows // groups
    folded = both[0:deep]
    for g in range(1, groups):
        folded = folded + pltpu.roll(both[g * deep : (g + 1) * deep], g * 2 * planes, 1)
    return folded


def unpack(folded, out, side, planes, rows):
    groups = lanes // (2 * planes)
    deep = rows // groups
    for g in range(groups):
        part = folded if g == 0 else pltpu.roll(folded, lanes - g * 2 * planes, 1)
        out[side, g * deep : (g + 1) * deep, :] = part


def beside(buf, beyond, i, r0, rows, planes, wide):
    y = buf[i, pl.ds(r0, rows + 2 * pad), :]
    tall = rows + 2 * pad
    c = y[pad : pad + rows]
    total = pltpu.roll(y, 1, 0)[pad : pad + rows] + pltpu.roll(y, tall - 1, 0)[pad : pad + rows]
    inner = pl.ds(r0 + pad, rows)
    total = total + buf[i - 1, inner, :] + buf[i + 1, inner, :]
    lane = lax.broadcasted_iota(jnp.int32, (rows, lanes), 1)
    left = pltpu.roll(beyond[0, pl.ds(r0, rows), :], 2 * lanes - planes - (i - 1), 1)
    right = pltpu.roll(beyond[1, pl.ds(r0, rows), :], lanes - 1 - (i - 1), 1)
    back = pltpu.roll(c, 1, 1)
    ahead = pltpu.roll(c, wide - 1, 1)
    first = jnp.where(lane == 0, left, back[:, 0:lanes])
    last = jnp.where(lane == lanes - 1, right, ahead[:, wide - lanes : wide])
    if wide > lanes:
        back = jnp.concatenate([first, back[:, lanes:]], axis=1)
        ahead = jnp.concatenate([ahead[:, : wide - lanes], last], axis=1)
    else:
        back, ahead = first, last
    return c, total + back + ahead


def advanced(c, around, spread, react):
    return c + spread * (around - 6.0 * c) + react * (c - c * c * c)


def halved(block, table, tmp):
    rows = block.shape[0]
    out = None
    rest = block
    for n in range(3):
        part = rest.astype(jnp.bfloat16)
        term = jnp.dot(part, table[...], preferred_element_type=jnp.float32)
        out = term if out is None else out + term
        if n < 2:
            rest = rest - part.astype(jnp.float32)
    tmp[...] = out
    return (tmp[pl.ds(0, rows // 2, stride=2), :] + tmp[pl.ds(1, rows // 2, stride=2), :]) * 0.125


def kernel(
    sizes, field, noise, obuf, kbuf,
    vbuf, mbuf, cbuf, n0, n1, pkv, pkm, pkc, hv, hm, hc, uv, um, uc, table, tmp,
    zs, zr, ls, lr, gs, gr, loc,
):
    nx, ny, nz = field.shape
    cx, cy, cz = nx // 2, ny // 2, nz // 2
    rows = ny // steps
    crows = rows // 2

    def ends(axis):
        me = lax.axis_index(axis)
        n = sizes[axis]
        return lax.rem(me + 1, n), lax.rem(me + n - 1, n)

    nxt = {a: ends(a)[0] for a in ("gz", "lvl", "gy")}
    prv = {a: ends(a)[1] for a in ("gz", "lvl", "gy")}

    load_v = pltpu.make_async_copy(field, vbuf.at[1 : nx + 1, pad : pad + ny, :], loc.at[0])
    load_n0 = pltpu.make_async_copy(noise.at[0], n0, loc.at[1])
    load_n1 = pltpu.make_async_copy(noise.at[1], n1, loc.at[2])
    load_v.start()
    load_n0.start()
    load_n1.start()

    barrier = pltpu.get_barrier_semaphore()
    for axis in ("gz", "lvl", "gy"):
        for side in (nxt, prv):
            pl.semaphore_signal(
                barrier, inc=1, device_id={axis: side[axis]}, device_id_type=pl.DeviceIdType.MESH
            )
    source = lax.broadcasted_iota(jnp.int32, (nz, cz), 0) // 2
    target = lax.broadcasted_iota(jnp.int32, (nz, cz), 1)
    table[...] = jnp.where(source == target, 1.0, 0.0).astype(jnp.bfloat16)
    pl.semaphore_wait(barrier, 6)

    def planes_out(src_low, src_high, buf, count, slot, where):
        up = remote(src_high, buf.at[(0,) + where], zs.at[0, slot], zr.at[0, slot], "gz", nxt["gz"])
        down = remote(src_low, buf.at[(count + 1,) + where], zs.at[1, slot], zr.at[1, slot], "gz", prv["gz"])
        up.start()
        down.start()
        return up, down

    def slabs_out(src_low, src_high, buf, count, tall, slot):
        up = remote(src_high, buf.at[1 : count + 1, 0:pad, :], gs.at[0, slot], gr.at[0, slot], "gy", nxt["gy"])
        down = remote(
            src_low, buf.at[1 : count + 1, pad + tall : 2 * pad + tall, :],
            gs.at[1, slot], gr.at[1, slot], "gy", prv["gy"],
        )
        up.start()
        down.start()
        return up, down

    def columns_out(packed, held, slot):
        up = remote(packed, held.at[0], ls.at[0, slot], lr.at[0, slot], "lvl", nxt["lvl"])
        down = remote(packed, held.at[1], ls.at[1, slot], lr.at[1, slot], "lvl", prv["lvl"])
        up.start()
        down.start()
        return up, down

    vz = []
    for c in range(steps):
        at = pl.ds(c * rows, rows)
        vz.append(
            planes_out(
                field.at[0, at, :], field.at[nx - 1, at, :], vbuf, nx, c, (pl.ds(pad + c * rows, rows), slice(None))
            )
        )
    vg = slabs_out(field.at[:, 0:pad, :], field.at[:, ny - pad : ny, :], vbuf, nx, ny, 0)

    load_v.wait()
    pkv[...] = pack(vbuf, nx, ny, nz)
    vl = columns_out(pkv, hv, 0)

    @pl.loop(0, cx * steps)
    def _(t):
        k, c = t // steps, t % steps
        at = pl.ds(pl.multiple_of(c * rows + pad, pad), rows)
        block = vbuf[2 * k + 1, at, :] + vbuf[2 * k + 2, at, :]
        cbuf[k + 1, pl.ds(pl.multiple_of(c * crows + pad, pad), crows), :] = halved(block, table, tmp)

    cin = (pl.ds(pad, cy), slice(None))
    cz_ = planes_out(cbuf.at[(1,) + cin], cbuf.at[(cx,) + cin], cbuf, cx, 2 * steps, cin)
    cg = slabs_out(cbuf.at[1 : cx + 1, pad : 2 * pad, :], cbuf.at[1 : cx + 1, cy : cy + pad, :], cbuf, cx, cy, 2)
    pkc[...] = pack(cbuf, cx, cy, cz)
    cl = columns_out(pkc, hc, 2)

    load_n0.wait()
    for copy in vg + vl:
        copy.wait_recv()
    for side in range(2):
        unpack(hv[side], uv, side, nx, ny)

    def middle(i, r0):
        c, around = beside(vbuf, uv, i, r0, rows, nx, nz)
        made = advanced(c, around, 0.15, 0.1) + noise_amp * n0[i - 1, pl.ds(r0, rows), :]
        mbuf[i, pl.ds(r0 + pad, rows), :] = made

    @pl.loop(0, (nx - 2) * steps)
    def _(t):
        middle(2 + t // steps, pl.multiple_of((t % steps) * rows, rows))

    mz = []
    for c in range(steps):
        for copy, i in zip(vz[c], (1, nx)):
            copy.wait_recv()
            middle(i, c * rows)
        where = (pl.ds(pad + c * rows, rows), slice(None))
        mz.append(planes_out(mbuf.at[(1,) + where], mbuf.at[(nx,) + where], mbuf, nx, steps + c, where))

    pkm[...] = pack(mbuf, nx, ny, nz)
    ml = columns_out(pkm, hm, 1)
    mg = slabs_out(mbuf.at[1 : nx + 1, pad : 2 * pad, :], mbuf.at[1 : nx + 1, ny : ny + pad, :], mbuf, nx, ny, 1)
    load_n1.wait()
    for copy in cz_ + cl + cg:
        copy.wait_recv()
    for side in range(2):
        unpack(hc[side], uc, side, cx, cy)
    for copy in ml + mg:
        copy.wait_recv()
    for side in range(2):
        unpack(hm[side], um, side, nx, ny)

    def finish(i, r0):
        c, around = beside(mbuf, um, i, r0, rows, nx, nz)
        made = advanced(c, around, 0.15, 0.1) + noise_amp * n1[i - 1, pl.ds(r0, rows), :]
        obuf[i - 1, pl.ds(r0, rows), :] = made

    def correct(k, r0, half):
        at = pl.ds(r0, rows)
        block = None
        for i in (2 * k, 2 * k + 1):
            term = obuf[i, at, :] - noise_amp * (n0[i, at, :] + n1[i, at, :])
            block = term if block is None else block + term
        c, around = beside(cbuf, uc, k + 1, half, crows, cx, cz)
        kbuf[k, pl.ds(half, crows), :] = halved(block, table, tmp) - advanced(c, around, 0.075, 0.2)

    @pl.loop(0, (nx - 2) * steps)
    def _(t):
        finish(2 + t // steps, pl.multiple_of((t % steps) * rows, rows))

    @pl.loop(0, (cx - 2) * steps)
    def _(t):
        c = t % steps
        correct(1 + t // steps, pl.multiple_of(c * rows, rows), pl.multiple_of(c * crows, crows))

    for c in range(steps):
        for side, i, k in ((0, 1, 0), (1, nx, cx - 1)):
            mz[c][side].wait_recv()
            finish(i, c * rows)
            correct(k, c * rows, c * crows)

    for group in vz + mz + [vg, vl, cz_, cg, cl, ml, mg]:
        for copy in group:
            copy.wait_send()


def put_out(fine, coarse, fine_out, coarse_out, sems):
    copies = [pltpu.make_async_copy(coarse, coarse_out, sems.at[0])]
    for i in range(fine.shape[0]):
        copies.append(pltpu.make_async_copy(fine.at[i], fine_out.at[i], sems.at[1 + i]))
    for copy in copies:
        copy.start()
    for copy in copies:
        copy.wait()


def on_device(sizes, fine_field, noise_pair):
    nx, ny, nz = fine_field.shape
    cx, cy, cz = nx // 2, ny // 2, nz // 2
    fold = ny // (lanes // (2 * nx))
    cfold = cy // (lanes // (2 * cx))
    f32 = jnp.float32
    whole = pl.BlockSpec(memory_space=pltpu.HBM)
    held = pl.BlockSpec(memory_space=pltpu.VMEM)
    dma = pltpu.SemaphoreType.DMA
    made = pl.pallas_call(
        functools.partial(kernel, sizes),
        out_shape=(jax.ShapeDtypeStruct((nx, ny, nz), f32), jax.ShapeDtypeStruct((cx, cy, cz), f32)),
        in_specs=[whole, whole],
        out_specs=(held, held),
        scratch_shapes=[
            pltpu.VMEM((nx + 2, ny + 2 * pad, nz), f32),
            pltpu.VMEM((nx + 2, ny + 2 * pad, nz), f32),
            pltpu.VMEM((cx + 2, cy + 2 * pad, cz), f32),
            pltpu.VMEM((nx, ny, nz), f32),
            pltpu.VMEM((nx, ny, nz), f32),
            pltpu.VMEM((fold, lanes), f32),
            pltpu.VMEM((fold, lanes), f32),
            pltpu.VMEM((cfold, lanes), f32),
            pltpu.VMEM((2, fold, lanes), f32),
            pltpu.VMEM((2, fold, lanes), f32),
            pltpu.VMEM((2, cfold, lanes), f32),
            pltpu.VMEM((2, ny, lanes), f32),
            pltpu.VMEM((2, ny, lanes), f32),
            pltpu.VMEM((2, cy, lanes), f32),
            pltpu.VMEM((nz, cz), jnp.bfloat16),
            pltpu.VMEM((ny // steps, cz), f32),
            dma((2, 2 * steps + 1)),
            dma((2, 2 * steps + 1)),
            dma((2, 3)),
            dma((2, 3)),
            dma((2, 3)),
            dma((2, 3)),
            dma((3,)),
        ],
        compiler_params=pltpu.CompilerParams(collective_id=0, has_side_effects=True, vmem_limit_bytes=50 * 2**20),
    )(fine_field, noise_pair)
    return pl.pallas_call(
        put_out,
        out_shape=(jax.ShapeDtypeStruct((nx, ny, nz), f32), jax.ShapeDtypeStruct((cx, cy, cz), f32)),
        in_specs=[held, held],
        out_specs=(whole, whole),
        scratch_shapes=[dma((nx + 1,))],
        compiler_params=pltpu.CompilerParams(vmem_limit_bytes=8 * 2**20),
    )(*made)


def solution(mesh):
    in_specs = (P("gz", "gy", "lvl"), P(None, "gz", "gy", "lvl"))
    out_specs = (P("gz", "gy", "lvl"), P("gz", "gy", "lvl"))
    sizes = dict(mesh.shape)
    return jax.shard_map(
        functools.partial(on_device, sizes), mesh=mesh, in_specs=in_specs, out_specs=out_specs, check_vma=False
    )
```

```python
import functools

import jax
import jax.numpy as jnp
from jax import lax
from jax.experimental import pallas as pl
from jax.experimental.pallas import tpu as pltpu
from jax.sharding import PartitionSpec as P

noise_amp = 0.3
lanes = 128
pad = 8
steps = 1


def remote(src, dst, send, recv, axis, where):
    return pltpu.make_async_remote_copy(
        src_ref=src,
        dst_ref=dst,
        send_sem=send,
        recv_sem=recv,
        device_id={axis: where},
        device_id_type=pl.DeviceIdType.MESH,
    )


def pack(buf, planes, rows, wide):
    lane = lax.broadcasted_iota(jnp.int32, (rows, lanes), 1)
    both = jnp.zeros((rows, lanes), jnp.float32)
    for i in range(planes):
        head = buf[1 + i, pad : pad + rows, 0:lanes]
        tail = buf[1 + i, pad : pad + rows, wide - lanes : wide]
        if i:
            head = pltpu.roll(head, i, 1)
        both = jnp.where(lane == i, head, both)
        both = jnp.where(lane == planes + i, pltpu.roll(tail, planes + i + 1, 1), both)
    groups = lanes // (2 * planes)
    deep = rows // groups
    folded = both[0:deep]
    for g in range(1, groups):
        folded = folded + pltpu.roll(both[g * deep : (g + 1) * deep], g * 2 * planes, 1)
    return folded


def unpack(folded, out, side, planes, rows):
    groups = lanes // (2 * planes)
    deep = rows // groups
    for g in range(groups):
        part = folded if g == 0 else pltpu.roll(folded, lanes - g * 2 * planes, 1)
        out[side, g * deep : (g + 1) * deep, :] = part


def beside(buf, beyond, i, r0, rows, planes, wide, lower=True, upper=True):
    y = buf[i, pl.ds(r0, rows + 2 * pad), :]
    tall = rows + 2 * pad
    c = y[pad : pad + rows]
    total = pltpu.roll(y, 1, 0)[pad : pad + rows] + pltpu.roll(y, tall - 1, 0)[pad : pad + rows]
    inner = pl.ds(r0 + pad, rows)
    if lower:
        total = total + buf[i - 1, inner, :]
    if upper:
        total = total + buf[i + 1, inner, :]
    lane = lax.broadcasted_iota(jnp.int32, (rows, lanes), 1)
    left = pltpu.roll(beyond[0, pl.ds(r0, rows), :], 2 * lanes - planes - (i - 1), 1)
    right = pltpu.roll(beyond[1, pl.ds(r0, rows), :], lanes - 1 - (i - 1), 1)
    back = pltpu.roll(c, 1, 1)
    ahead = pltpu.roll(c, wide - 1, 1)
    first = jnp.where(lane == 0, left, back[:, 0:lanes])
    last = jnp.where(lane == lanes - 1, right, ahead[:, wide - lanes : wide])
    if wide > lanes:
        back = jnp.concatenate([first, back[:, lanes:]], axis=1)
        ahead = jnp.concatenate([ahead[:, : wide - lanes], last], axis=1)
    else:
        back, ahead = first, last
    return c, total + back + ahead


def advanced(c, around, spread, react):
    return c + spread * (around - 6.0 * c) + react * (c - c * c * c)


def halved(block, table, tmp):
    rows = block.shape[0]
    out = None
    rest = block
    for n in range(3):
        part = rest.astype(jnp.bfloat16)
        term = jnp.dot(part, table[...], preferred_element_type=jnp.float32)
        out = term if out is None else out + term
        if n < 2:
            rest = rest - part.astype(jnp.float32)
    tmp[0:rows, :] = out
    return (tmp[pl.ds(0, rows // 2, stride=2), :] + tmp[pl.ds(1, rows // 2, stride=2), :]) * 0.125


def kernel(
    sizes, field, noise, obuf, kbuf,
    vbuf, mbuf, cbuf, n0, n1, pkv, pkm, pkc, hv, hm, hc, uv, um, uc, table, tmp,
    zs, zr, ls, lr, gs, gr, loc,
):
    nx, ny, nz = field.shape
    cx, cy, cz = nx // 2, ny // 2, nz // 2
    rows = ny // steps
    crows = rows // 2

    def ends(axis):
        me = lax.axis_index(axis)
        n = sizes[axis]
        return lax.rem(me + 1, n), lax.rem(me + n - 1, n)

    nxt = {a: ends(a)[0] for a in ("gz", "lvl", "gy")}
    prv = {a: ends(a)[1] for a in ("gz", "lvl", "gy")}

    load_v = pltpu.make_async_copy(field, vbuf.at[1 : nx + 1, pad : pad + ny, :], loc.at[0])
    load_n0 = pltpu.make_async_copy(noise.at[0], n0, loc.at[1])
    load_n1 = pltpu.make_async_copy(noise.at[1], n1, loc.at[2])
    load_v.start()
    load_n0.start()
    load_n1.start()

    barrier = pltpu.get_barrier_semaphore()
    for axis in ("gz", "lvl", "gy"):
        for side in (nxt, prv):
            pl.semaphore_signal(
                barrier, inc=1, device_id={axis: side[axis]}, device_id_type=pl.DeviceIdType.MESH
            )
    source = lax.broadcasted_iota(jnp.int32, (nz, cz), 0) // 2
    target = lax.broadcasted_iota(jnp.int32, (nz, cz), 1)
    table[...] = jnp.where(source == target, 1.0, 0.0).astype(jnp.bfloat16)
    pl.semaphore_wait(barrier, 6)

    def planes_up(src, buf, count, slot, where):
        up = remote(src, buf.at[(0,) + where], zs.at[0, slot], zr.at[0, slot], "gz", nxt["gz"])
        up.start()
        return up

    def planes_down(src, buf, count, slot, where):
        down = remote(src, buf.at[(count + 1,) + where], zs.at[1, slot], zr.at[1, slot], "gz", prv["gz"])
        down.start()
        return down

    def planes_out(src_low, src_high, *rest):
        return planes_up(src_high, *rest), planes_down(src_low, *rest)

    def slabs_out(src_low, src_high, buf, count, tall, slot):
        up = remote(src_high, buf.at[1 : count + 1, 0:pad, :], gs.at[0, slot], gr.at[0, slot], "gy", nxt["gy"])
        down = remote(
            src_low, buf.at[1 : count + 1, pad + tall : 2 * pad + tall, :],
            gs.at[1, slot], gr.at[1, slot], "gy", prv["gy"],
        )
        up.start()
        down.start()
        return up, down

    def columns_out(packed, held, slot):
        up = remote(packed, held.at[0], ls.at[0, slot], lr.at[0, slot], "lvl", nxt["lvl"])
        down = remote(packed, held.at[1], ls.at[1, slot], lr.at[1, slot], "lvl", prv["lvl"])
        up.start()
        down.start()
        return up, down

    vz = []
    for c in range(steps):
        at = pl.ds(c * rows, rows)
        vz.append(
            planes_out(
                field.at[0, at, :], field.at[nx - 1, at, :], vbuf, nx, c, (pl.ds(pad + c * rows, rows), slice(None))
            )
        )
    vg = slabs_out(field.at[:, 0:pad, :], field.at[:, ny - pad : ny, :], vbuf, nx, ny, 0)

    load_v.wait()
    pkv[...] = pack(vbuf, nx, ny, nz)
    vl = columns_out(pkv, hv, 0)

    @pl.loop(0, cx)
    def _(k):
        block = vbuf[2 * k + 1, pad : pad + ny, :] + vbuf[2 * k + 2, pad : pad + ny, :]
        cbuf[k + 1, pad : pad + cy, :] = halved(block, table, tmp)

    cin = (pl.ds(pad, cy), slice(None))
    cz_ = planes_out(cbuf.at[(1,) + cin], cbuf.at[(cx,) + cin], cbuf, cx, 2 * steps, cin)
    cg = slabs_out(cbuf.at[1 : cx + 1, pad : 2 * pad, :], cbuf.at[1 : cx + 1, cy : cy + pad, :], cbuf, cx, cy, 2)
    pkc[...] = pack(cbuf, cx, cy, cz)
    cl = columns_out(pkc, hc, 2)

    load_n0.wait()
    for copy in vg + vl:
        copy.wait_recv()
    for side in range(2):
        unpack(hv[side], uv, side, nx, ny)

    def middle(i, r0, rows):
        c, around = beside(vbuf, uv, i, r0, rows, nx, nz)
        made = advanced(c, around, 0.15, 0.1) + noise_amp * n0[i - 1, pl.ds(r0, rows), :]
        mbuf[i, pl.ds(r0 + pad, rows), :] = made

    @pl.loop(0, nx - 2)
    def _(t):
        middle(2 + t, 0, ny)

    mz = []
    for s in range(steps):
        where = (pl.ds(pad + s * rows, rows), slice(None))
        pair = []
        for copy, i, gone in zip(vz[s][::-1], (nx, 1), (planes_up, planes_down)):
            copy.wait_recv()
            middle(i, s * rows, rows)
            pair.append(gone(mbuf.at[(i,) + where], mbuf, nx, steps + s, where))
        mz.append((pair[0], pair[1]))

    pkm[...] = pack(mbuf, nx, ny, nz)
    ml = columns_out(pkm, hm, 1)
    mg = slabs_out(mbuf.at[1 : nx + 1, pad : 2 * pad, :], mbuf.at[1 : nx + 1, ny : ny + pad, :], mbuf, nx, ny, 1)
    load_n1.wait()
    for copy in cz_ + cl + cg:
        copy.wait_recv()
    for side in range(2):
        unpack(hc[side], uc, side, cx, cy)
    for copy in ml + mg:
        copy.wait_recv()
    for side in range(2):
        unpack(hm[side], um, side, nx, ny)

    def finish(i, lower=True, upper=True):
        c, around = beside(mbuf, um, i, 0, ny, nx, nz, lower, upper)
        obuf[i - 1] = advanced(c, around, 0.15, 0.1) + noise_amp * n1[i - 1]

    def correct(k):
        block = None
        for i in (2 * k, 2 * k + 1):
            term = obuf[i] - noise_amp * (n0[i] + n1[i])
            block = term if block is None else block + term
        c, around = beside(cbuf, uc, k + 1, 0, cy, cx, cz)
        kbuf[k] = halved(block, table, tmp) - advanced(c, around, 0.075, 0.2)

    @pl.loop(2, nx)
    def _(i):
        finish(i)

    finish(1, lower=False)
    finish(nx, upper=False)

    @pl.loop(0, cx)
    def _(k):
        correct(k)

    for s in range(steps):
        for side, i, k, beyond in ((0, 0, 0, 0), (1, nx - 1, cx - 1, nx + 1)):
            mz[s][side].wait_recv()
            at, low = pl.ds(s * rows, rows), pl.ds(s * crows, crows)
            more = 0.15 * mbuf[beyond, pl.ds(pad + s * rows, rows), :]
            obuf[i, at, :] = obuf[i, at, :] + more
            kbuf[k, low, :] = kbuf[k, low, :] + halved(more, table, tmp)

    for group in vz + mz + [vg, vl, cz_, cg, cl, ml, mg]:
        for copy in group:
            copy.wait_send()


def put_out(fine, coarse, fine_out, coarse_out, sems):
    copies = [pltpu.make_async_copy(coarse, coarse_out, sems.at[0])]
    for i in range(fine.shape[0]):
        copies.append(pltpu.make_async_copy(fine.at[i], fine_out.at[i], sems.at[1 + i]))
    for copy in copies:
        copy.start()
    for copy in copies:
        copy.wait()


def on_device(sizes, fine_field, noise_pair):
    nx, ny, nz = fine_field.shape
    cx, cy, cz = nx // 2, ny // 2, nz // 2
    fold = ny // (lanes // (2 * nx))
    cfold = cy // (lanes // (2 * cx))
    f32 = jnp.float32
    whole = pl.BlockSpec(memory_space=pltpu.HBM)
    held = pl.BlockSpec(memory_space=pltpu.VMEM)
    dma = pltpu.SemaphoreType.DMA
    made = pl.pallas_call(
        functools.partial(kernel, sizes),
        out_shape=(jax.ShapeDtypeStruct((nx, ny, nz), f32), jax.ShapeDtypeStruct((cx, cy, cz), f32)),
        in_specs=[whole, whole],
        out_specs=(held, held),
        scratch_shapes=[
            pltpu.VMEM((nx + 2, ny + 2 * pad, nz), f32),
            pltpu.VMEM((nx + 2, ny + 2 * pad, nz), f32),
            pltpu.VMEM((cx + 2, cy + 2 * pad, cz), f32),
            pltpu.VMEM((nx, ny, nz), f32),
            pltpu.VMEM((nx, ny, nz), f32),
            pltpu.VMEM((fold, lanes), f32),
            pltpu.VMEM((fold, lanes), f32),
            pltpu.VMEM((cfold, lanes), f32),
            pltpu.VMEM((2, fold, lanes), f32),
            pltpu.VMEM((2, fold, lanes), f32),
            pltpu.VMEM((2, cfold, lanes), f32),
            pltpu.VMEM((2, ny, lanes), f32),
            pltpu.VMEM((2, ny, lanes), f32),
            pltpu.VMEM((2, cy, lanes), f32),
            pltpu.VMEM((nz, cz), jnp.bfloat16),
            pltpu.VMEM((ny, cz), f32),
            dma((2, 2 * steps + 1)),
            dma((2, 2 * steps + 1)),
            dma((2, 3)),
            dma((2, 3)),
            dma((2, 3)),
            dma((2, 3)),
            dma((3,)),
        ],
        compiler_params=pltpu.CompilerParams(collective_id=0, has_side_effects=True, vmem_limit_bytes=50 * 2**20),
    )(fine_field, noise_pair)
    return pl.pallas_call(
        put_out,
        out_shape=(jax.ShapeDtypeStruct((nx, ny, nz), f32), jax.ShapeDtypeStruct((cx, cy, cz), f32)),
        in_specs=[held, held],
        out_specs=(whole, whole),
        scratch_shapes=[dma((nx + 1,))],
        compiler_params=pltpu.CompilerParams(vmem_limit_bytes=8 * 2**20),
    )(*made)


def solution(mesh):
    in_specs = (P("gz", "gy", "lvl"), P(None, "gz", "gy", "lvl"))
    out_specs = (P("gz", "gy", "lvl"), P("gz", "gy", "lvl"))
    sizes = dict(mesh.shape)
    return jax.shard_map(
        functools.partial(on_device, sizes), mesh=mesh, in_specs=in_specs, out_specs=out_specs, check_vma=False
    )
```

```python
import functools

import jax
import jax.numpy as jnp
from jax import lax
from jax.experimental import pallas as pl
from jax.experimental.pallas import tpu as pltpu
from jax.sharding import PartitionSpec as P

noise_amp = 0.3
lanes = 128
pad = 8
steps = 1


def remote(src, dst, send, recv, axis, where):
    return pltpu.make_async_remote_copy(
        src_ref=src,
        dst_ref=dst,
        send_sem=send,
        recv_sem=recv,
        device_id={axis: where},
        device_id_type=pl.DeviceIdType.MESH,
    )


def pack(buf, planes, rows, wide):
    lane = lax.broadcasted_iota(jnp.int32, (rows, lanes), 1)
    both = jnp.zeros((rows, lanes), jnp.float32)
    for i in range(planes):
        head = buf[1 + i, pad : pad + rows, 0:lanes]
        tail = buf[1 + i, pad : pad + rows, wide - lanes : wide]
        if i:
            head = pltpu.roll(head, i, 1)
        both = jnp.where(lane == i, head, both)
        both = jnp.where(lane == planes + i, pltpu.roll(tail, planes + i + 1, 1), both)
    groups = lanes // (2 * planes)
    deep = rows // groups
    folded = both[0:deep]
    for g in range(1, groups):
        folded = folded + pltpu.roll(both[g * deep : (g + 1) * deep], g * 2 * planes, 1)
    return folded


def unpack(folded, out, side, planes, rows):
    groups = lanes // (2 * planes)
    deep = rows // groups
    for g in range(groups):
        part = folded if g == 0 else pltpu.roll(folded, lanes - g * 2 * planes, 1)
        out[side, g * deep : (g + 1) * deep, :] = part


def beside(buf, beyond, i, r0, rows, planes, wide, lower=True, upper=True):
    y = buf[i, pl.ds(r0, rows + 2 * pad), :]
    tall = rows + 2 * pad
    c = y[pad : pad + rows]
    total = pltpu.roll(y, 1, 0)[pad : pad + rows] + pltpu.roll(y, tall - 1, 0)[pad : pad + rows]
    inner = pl.ds(r0 + pad, rows)
    if lower:
        total = total + buf[i - 1, inner, :]
    if upper:
        total = total + buf[i + 1, inner, :]
    lane = lax.broadcasted_iota(jnp.int32, (rows, lanes), 1)
    left = pltpu.roll(beyond[0, pl.ds(r0, rows), :], 2 * lanes - planes - (i - 1), 1)
    right = pltpu.roll(beyond[1, pl.ds(r0, rows), :], lanes - 1 - (i - 1), 1)
    back = pltpu.roll(c, 1, 1)
    ahead = pltpu.roll(c, wide - 1, 1)
    first = jnp.where(lane == 0, left, back[:, 0:lanes])
    last = jnp.where(lane == lanes - 1, right, ahead[:, wide - lanes : wide])
    if wide > lanes:
        back = jnp.concatenate([first, back[:, lanes:]], axis=1)
        ahead = jnp.concatenate([ahead[:, : wide - lanes], last], axis=1)
    else:
        back, ahead = first, last
    return c, total + back + ahead


def advanced(c, around, spread, react):
    return c + spread * (around - 6.0 * c) + react * (c - c * c * c)


def halved(block, table, tmp):
    rows = block.shape[0]
    out = None
    rest = block
    for n in range(3):
        part = rest.astype(jnp.bfloat16)
        term = jnp.dot(part, table[...], preferred_element_type=jnp.float32)
        out = term if out is None else out + term
        if n < 2:
            rest = rest - part.astype(jnp.float32)
    tmp[0:rows, :] = out
    return (tmp[pl.ds(0, rows // 2, stride=2), :] + tmp[pl.ds(1, rows // 2, stride=2), :]) * 0.125


def kernel(
    sizes, field, noise, obuf, kbuf,
    vbuf, mbuf, cbuf, n0, n1, pkv, pkm, pkc, hv, hm, hc, uv, um, uc, table, tmp,
    zs, zr, ls, lr, gs, gr, loc,
):
    nx, ny, nz = field.shape
    cx, cy, cz = nx // 2, ny // 2, nz // 2
    rows = ny // steps
    crows = rows // 2

    def ends(axis):
        me = lax.axis_index(axis)
        n = sizes[axis]
        return lax.rem(me + 1, n), lax.rem(me + n - 1, n)

    nxt = {a: ends(a)[0] for a in ("gz", "lvl", "gy")}
    prv = {a: ends(a)[1] for a in ("gz", "lvl", "gy")}

    barrier = pltpu.get_barrier_semaphore()
    for axis in ("gz", "lvl", "gy"):
        for side in (nxt, prv):
            pl.semaphore_signal(
                barrier, inc=1, device_id={axis: side[axis]}, device_id_type=pl.DeviceIdType.MESH
            )
    load_v = pltpu.make_async_copy(field, vbuf.at[1 : nx + 1, pad : pad + ny, :], loc.at[0])
    load_n0 = pltpu.make_async_copy(noise.at[0], n0, loc.at[1])
    load_n1 = pltpu.make_async_copy(noise.at[1], n1, loc.at[2])
    load_v.start()
    load_n0.start()
    load_n1.start()

    source = lax.broadcasted_iota(jnp.int32, (nz, cz), 0) // 2
    target = lax.broadcasted_iota(jnp.int32, (nz, cz), 1)
    table[...] = jnp.where(source == target, 1.0, 0.0).astype(jnp.bfloat16)
    pl.semaphore_wait(barrier, 6)

    def planes_up(src, buf, count, slot, where):
        up = remote(src, buf.at[(0,) + where], zs.at[0, slot], zr.at[0, slot], "gz", nxt["gz"])
        up.start()
        return up

    def planes_down(src, buf, count, slot, where):
        down = remote(src, buf.at[(count + 1,) + where], zs.at[1, slot], zr.at[1, slot], "gz", prv["gz"])
        down.start()
        return down

    def planes_out(src_low, src_high, *rest):
        return planes_up(src_high, *rest), planes_down(src_low, *rest)

    def slabs_out(src_low, src_high, buf, count, tall, slot):
        up = remote(src_high, buf.at[1 : count + 1, 0:pad, :], gs.at[0, slot], gr.at[0, slot], "gy", nxt["gy"])
        down = remote(
            src_low, buf.at[1 : count + 1, pad + tall : 2 * pad + tall, :],
            gs.at[1, slot], gr.at[1, slot], "gy", prv["gy"],
        )
        up.start()
        down.start()
        return up, down

    def columns_out(packed, held, slot):
        up = remote(packed, held.at[0], ls.at[0, slot], lr.at[0, slot], "lvl", nxt["lvl"])
        down = remote(packed, held.at[1], ls.at[1, slot], lr.at[1, slot], "lvl", prv["lvl"])
        up.start()
        down.start()
        return up, down

    vz = []
    for c in range(steps):
        at = pl.ds(c * rows, rows)
        vz.append(
            planes_out(
                field.at[0, at, :], field.at[nx - 1, at, :], vbuf, nx, c, (pl.ds(pad + c * rows, rows), slice(None))
            )
        )
    vg = slabs_out(field.at[:, 0:pad, :], field.at[:, ny - pad : ny, :], vbuf, nx, ny, 0)

    load_v.wait()
    pkv[...] = pack(vbuf, nx, ny, nz)
    vl = columns_out(pkv, hv, 0)

    @pl.loop(0, cx)
    def _(k):
        block = vbuf[2 * k + 1, pad : pad + ny, :] + vbuf[2 * k + 2, pad : pad + ny, :]
        cbuf[k + 1, pad : pad + cy, :] = halved(block, table, tmp)

    cin = (pl.ds(pad, cy), slice(None))
    cz_ = planes_out(cbuf.at[(1,) + cin], cbuf.at[(cx,) + cin], cbuf, cx, 2 * steps, cin)
    cg = slabs_out(cbuf.at[1 : cx + 1, pad : 2 * pad, :], cbuf.at[1 : cx + 1, cy : cy + pad, :], cbuf, cx, cy, 2)
    pkc[...] = pack(cbuf, cx, cy, cz)
    cl = columns_out(pkc, hc, 2)

    load_n0.wait()
    for copy in vg + vl:
        copy.wait_recv()
    for side in range(2):
        unpack(hv[side], uv, side, nx, ny)

    def middle(i, r0, rows):
        c, around = beside(vbuf, uv, i, r0, rows, nx, nz)
        made = advanced(c, around, 0.15, 0.1) + noise_amp * n0[i - 1, pl.ds(r0, rows), :]
        mbuf[i, pl.ds(r0 + pad, rows), :] = made

    @pl.loop(0, nx - 2)
    def _(t):
        middle(2 + t, 0, ny)

    mz = []
    for s in range(steps):
        where = (pl.ds(pad + s * rows, rows), slice(None))
        pair = []
        for copy, i, gone in zip(vz[s][::-1], (nx, 1), (planes_up, planes_down)):
            copy.wait_recv()
            middle(i, s * rows, rows)
            pair.append(gone(mbuf.at[(i,) + where], mbuf, nx, steps + s, where))
        mz.append((pair[0], pair[1]))

    pkm[...] = pack(mbuf, nx, ny, nz)
    ml = columns_out(pkm, hm, 1)
    mg = slabs_out(mbuf.at[1 : nx + 1, pad : 2 * pad, :], mbuf.at[1 : nx + 1, ny : ny + pad, :], mbuf, nx, ny, 1)
    load_n1.wait()
    for copy in cz_ + cl + cg:
        copy.wait_recv()
    for side in range(2):
        unpack(hc[side], uc, side, cx, cy)
    for copy in ml + mg:
        copy.wait_recv()
    for side in range(2):
        unpack(hm[side], um, side, nx, ny)

    def finish(i, lower=True, upper=True):
        c, around = beside(mbuf, um, i, 0, ny, nx, nz, lower, upper)
        obuf[i - 1] = advanced(c, around, 0.15, 0.1) + noise_amp * n1[i - 1]

    def correct(k):
        block = None
        for i in (2 * k, 2 * k + 1):
            term = obuf[i] - noise_amp * (n0[i] + n1[i])
            block = term if block is None else block + term
        c, around = beside(cbuf, uc, k + 1, 0, cy, cx, cz)
        kbuf[k] = halved(block, table, tmp) - advanced(c, around, 0.075, 0.2)

    @pl.loop(2, nx)
    def _(i):
        finish(i)

    finish(1, lower=False)
    finish(nx, upper=False)

    @pl.loop(0, cx)
    def _(k):
        correct(k)

    for s in range(steps):
        for side, i, k, beyond in ((0, 0, 0, 0), (1, nx - 1, cx - 1, nx + 1)):
            mz[s][side].wait_recv()
            at, low = pl.ds(s * rows, rows), pl.ds(s * crows, crows)
            more = 0.15 * mbuf[beyond, pl.ds(pad + s * rows, rows), :]
            obuf[i, at, :] = obuf[i, at, :] + more
            kbuf[k, low, :] = kbuf[k, low, :] + halved(more, table, tmp)

    for group in vz + mz + [vg, vl, cz_, cg, cl, ml, mg]:
        for copy in group:
            copy.wait_send()


def put_out(fine, coarse, fine_out, coarse_out, sems):
    copies = [pltpu.make_async_copy(coarse, coarse_out, sems.at[0])]
    for i in range(fine.shape[0]):
        copies.append(pltpu.make_async_copy(fine.at[i], fine_out.at[i], sems.at[1 + i]))
    for copy in copies:
        copy.start()
    for copy in copies:
        copy.wait()


def on_device(sizes, fine_field, noise_pair):
    nx, ny, nz = fine_field.shape
    cx, cy, cz = nx // 2, ny // 2, nz // 2
    fold = ny // (lanes // (2 * nx))
    cfold = cy // (lanes // (2 * cx))
    f32 = jnp.float32
    whole = pl.BlockSpec(memory_space=pltpu.HBM)
    held = pl.BlockSpec(memory_space=pltpu.VMEM)
    dma = pltpu.SemaphoreType.DMA
    made = pl.pallas_call(
        functools.partial(kernel, sizes),
        out_shape=(jax.ShapeDtypeStruct((nx, ny, nz), f32), jax.ShapeDtypeStruct((cx, cy, cz), f32)),
        in_specs=[whole, whole],
        out_specs=(held, held),
        scratch_shapes=[
            pltpu.VMEM((nx + 2, ny + 2 * pad, nz), f32),
            pltpu.VMEM((nx + 2, ny + 2 * pad, nz), f32),
            pltpu.VMEM((cx + 2, cy + 2 * pad, cz), f32),
            pltpu.VMEM((nx, ny, nz), f32),
            pltpu.VMEM((nx, ny, nz), f32),
            pltpu.VMEM((fold, lanes), f32),
            pltpu.VMEM((fold, lanes), f32),
            pltpu.VMEM((cfold, lanes), f32),
            pltpu.VMEM((2, fold, lanes), f32),
            pltpu.VMEM((2, fold, lanes), f32),
            pltpu.VMEM((2, cfold, lanes), f32),
            pltpu.VMEM((2, ny, lanes), f32),
            pltpu.VMEM((2, ny, lanes), f32),
            pltpu.VMEM((2, cy, lanes), f32),
            pltpu.VMEM((nz, cz), jnp.bfloat16),
            pltpu.VMEM((ny + pad, cz), f32),
            dma((2, 2 * steps + 1)),
            dma((2, 2 * steps + 1)),
            dma((2, 3)),
            dma((2, 3)),
            dma((2, 3)),
            dma((2, 3)),
            dma((3,)),
        ],
        compiler_params=pltpu.CompilerParams(collective_id=0, has_side_effects=True, vmem_limit_bytes=50 * 2**20),
    )(fine_field, noise_pair)
    return pl.pallas_call(
        put_out,
        out_shape=(jax.ShapeDtypeStruct((nx, ny, nz), f32), jax.ShapeDtypeStruct((cx, cy, cz), f32)),
        in_specs=[held, held],
        out_specs=(whole, whole),
        scratch_shapes=[dma((nx + 1,))],
        compiler_params=pltpu.CompilerParams(vmem_limit_bytes=8 * 2**20),
    )(*made)


def solution(mesh):
    in_specs = (P("gz", "gy", "lvl"), P(None, "gz", "gy", "lvl"))
    out_specs = (P("gz", "gy", "lvl"), P("gz", "gy", "lvl"))
    sizes = dict(mesh.shape)
    return jax.shard_map(
        functools.partial(on_device, sizes), mesh=mesh, in_specs=in_specs, out_specs=out_specs, check_vma=False
    )
```
